32 devices in a mesh: dom: 8 (over z, core), rep: 4 (over y, x).
Axes of the slice: x: 2, y: 2, z: 4, core: 2. Of those that a mesh axis runs over, the one named last changes fastest.
Arguments:
- node_features: bfloat16 [16384, 256], P(('dom', 'rep')), may hold values from -6 to 6
- weight: bfloat16 [256, 256], replicated, may hold values from -0.375 to 0.375
- cotangent: bfloat16 [16384, 256], P(('dom', 'rep')), may hold values from -6 to 6
- tile_row: int32 [8, 4, 512], P('dom', 'rep'), may hold values from 0 to 15
- tile_col: int32 [8, 4, 512], P('dom', 'rep'), may hold values from 0 to 31
- tile_values: bfloat16 [8, 4, 512, 128, 128], P('dom', 'rep'), may hold values from -0.0625 to 0.0625
- tile_count: int32 [8, 4], P('dom', 'rep'), may hold values from 128 to 512, as said below
Outputs:
- output: bfloat16 [16384, 256], P(('dom', 'rep'))
- grad_features: bfloat16 [16384, 256], P(('dom', 'rep'))
- grad_weight: float32 [256, 256], replicated
The draws below stay inside these ranges and needn't reach their ends.
Inputs may be any that keep to these rules, and one draw needn't show every extreme that they name: Live slots are the first tile_count slots of each device's list; some device has all 512 slots live.
All inputs are finite; a program needn't handle non-finite values.
Results may differ from the reference program's by a relative error of at most 0.0061.
Values may be sent and summed in bfloat16 or wider, within the bound.
A program may use at most 192 MiB of HBM per device.

```python
import jax
import jax.numpy as jnp
from jax import lax

F = 256
S = 4
K = 512
NODES = 16384
N_DOM = 8
N_REP = 4


def draw_tile_count(key, part):
    counts = jax.random.randint(jax.random.fold_in(key, 11), (N_DOM * N_REP,), K // 4, K + 1)
    fullest = jax.random.randint(jax.random.fold_in(key, 12), (), 0, N_DOM * N_REP)
    counts = jnp.where(jnp.arange(N_DOM * N_REP) == fullest, K, counts)
    return counts.reshape(N_DOM, N_REP).astype(jnp.int32)


def place_ends(drawn, key, least, largest):
    longest = drawn.shape.index(max(drawn.shape))
    spots = []
    for shift in (0, 1):
        where = [jax.random.randint(jax.random.fold_in(key, axis), (), 0, length) for axis, length in enumerate(drawn.shape)]
        where[longest] = (where[longest] + shift) % drawn.shape[longest]
        spots.append(tuple(where))
    return drawn.at[spots[0]].set(least).at[spots[1]].set(largest)


def steps_of(stream_key, shape, pieces, least, largest):
    loudness, own = 1.0, jax.random.fold_in(stream_key, 6)
    for position, parts in pieces:
        steps = jnp.exp(jax.random.uniform(jax.random.fold_in(own, position), (parts,), jnp.float32, least / len(pieces), largest / len(pieces)))
        loudness = loudness * jnp.repeat(steps, shape[position] // parts).reshape([-1 if axis == position else 1 for axis in range(len(shape))])
    return loudness


def centred(key, shape, deviation, reach, split=(), held_as=jnp.bfloat16):
    gain = steps_of(key, shape, split, -0.22, 0.18) if split else 1.0
    result = jax.random.normal(key, shape, jnp.float32) * deviation * gain
    return jnp.minimum(jnp.maximum(result, -reach), reach).astype(held_as)


def setup_inputs(seed: int = 0) -> dict:
    streams_of = jax.random.split(jax.random.key(seed), 8)
    node_features = centred(streams_of[0], (NODES, F), 1.0, 6.0, ((0, 32),))
    weight = centred(streams_of[1], (F, F), F ** -0.5, 0.375)
    cotangent = centred(streams_of[2], (NODES, F), 1.0, 6.0, ((0, 32),))
    tile_row = place_ends(jax.random.randint(streams_of[3], (N_DOM, N_REP, K), 0, N_REP * S), jax.random.fold_in(streams_of[3], 1), 0, (N_REP * S) - 1).astype(jnp.int32)
    tile_col = place_ends(jax.random.randint(streams_of[4], (N_DOM, N_REP, K), 0, N_DOM * S), jax.random.fold_in(streams_of[4], 1), 0, (N_DOM * S) - 1).astype(jnp.int32)
    tile_values = centred(streams_of[5], (N_DOM, N_REP, K, 128, 128), (16 * K) ** -0.5, 0.0625, ((0, 8), (1, 4)))
    tile_count = draw_tile_count(jax.random.fold_in(streams_of[7], 71), 0)
    return dict(node_features=node_features, weight=weight, cotangent=cotangent, tile_row=tile_row, tile_col=tile_col, tile_values=tile_values, tile_count=tile_count)


def silu_slope(summed):
    sig = jax.nn.sigmoid(summed)
    return sig * (1.0 + summed * (1.0 - sig))


def spread(source, values, pick, place, active, flipped, total_blocks):
    pattern = "tba,tbf->taf" if flipped else "tab,tbf->taf"

    def one_device(accum, items):
        tiles, pick_index, place_index, enabled = items
        picked = source[pick_index].astype(jnp.float32)
        products = jnp.einsum(pattern, tiles.astype(jnp.float32), picked)
        products = products * enabled.astype(jnp.float32)[:, None, None]
        return accum.at[place_index].add(products), None

    start = jnp.zeros((total_blocks, 128, source.shape[2]), jnp.float32)
    accum, unused = lax.scan(one_device, start, (values, pick, place, active))
    return accum


def reference(node_features, weight, cotangent, tile_row, tile_col, tile_values, tile_count):
    blocks_part = N_REP * S
    total_blocks = NODES // 128
    projected = jnp.dot(node_features, weight, preferred_element_type=jnp.float32).astype(jnp.bfloat16)
    source = projected.reshape(total_blocks, 128, F)
    part_index = jnp.arange(N_DOM, dtype=jnp.int32)[:, None, None]
    repl_index = jnp.arange(N_REP, dtype=jnp.int32)[None, :, None]
    global_row = (part_index * blocks_part + tile_row).reshape(N_DOM * N_REP, K).astype(jnp.int32)
    global_col = ((tile_col // S) * blocks_part + repl_index * S + tile_col % S).reshape(N_DOM * N_REP, K).astype(jnp.int32)
    active = (jnp.arange(K, dtype=jnp.int32)[None, None, :] < tile_count[:, :, None]).reshape(N_DOM * N_REP, K)
    values = tile_values.reshape(N_DOM * N_REP, K, 128, 128)
    summed = spread(source, values, global_col, global_row, active, False, total_blocks).reshape(NODES, F)
    output = jax.nn.silu(summed).astype(jnp.bfloat16)
    grad_summed = (cotangent.astype(jnp.float32) * silu_slope(summed)).astype(jnp.bfloat16)
    back = spread(grad_summed.reshape(total_blocks, 128, F), values, global_row, global_col, active, True, total_blocks)
    grad_projected = back.reshape(NODES, F).astype(jnp.bfloat16)
    grad_features = jnp.dot(grad_projected, weight.T, preferred_element_type=jnp.float32).astype(jnp.bfloat16)
    grad_weight = jnp.dot(node_features.T, grad_projected, preferred_element_type=jnp.float32)
    return output, grad_features, grad_weight
```

```python
import functools

import jax
import jax.numpy as jnp
from jax import lax
from jax.experimental import pallas as pl
from jax.experimental.pallas import tpu as pltpu
from jax.sharding import PartitionSpec as P

LOADS = 8
SUB = 2
SPLIT = 4
TILE = 128
MESH = pl.DeviceIdType.MESH


def order_tiles(count, row, col, col_blocks, order_out, place_out, last_out):
    slots, places = order_out.shape[1], last_out.shape[1]
    square = (TILE, TILE)
    lane = lax.broadcasted_iota(jnp.int32, (1, slots), 1)
    spot = jnp.where(lane < count, row * col_blocks + col, places)
    key = (spot * slots + lane).astype(jnp.float32)
    spot = spot.astype(jnp.float32)
    across = lax.broadcasted_iota(jnp.int32, square, 1).astype(jnp.float32)
    down = lax.broadcasted_iota(jnp.int32, square, 0).astype(jnp.float32)
    ones = jnp.ones(square, jnp.bfloat16)
    groups = slots // TILE
    zero = jnp.zeros(square, jnp.float32)

    def wide(values, q):
        return jnp.broadcast_to(values[:, q * TILE : (q + 1) * TILE], square)

    tall_spot, rank = [], []
    for q in range(groups):
        tall_key = jnp.transpose(wide(key, q))
        tall_spot.append(jnp.transpose(wide(spot, q)))
        ahead = zero
        for j in range(groups):
            ahead = ahead + jnp.where(wide(key, j) < tall_key, 1.0, 0.0)
        rank.append(jnp.dot(ahead.astype(jnp.bfloat16), ones, preferred_element_type=jnp.float32))
    for r in range(groups):
        want = across + float(r * TILE)
        slot, place = zero, zero
        for q in range(groups):
            hit = rank[q] == want
            slot = slot + jnp.where(hit, down + float(q * TILE), 0.0)
            place = place + jnp.where(hit, tall_spot[q], 0.0)
        order_out[:, pl.ds(r * TILE, TILE)] = jnp.sum(slot, axis=0, keepdims=True).astype(jnp.int32)
        place_out[:, pl.ds(r * TILE, TILE)] = jnp.sum(place, axis=0, keepdims=True).astype(jnp.int32)
    for p in range(places // TILE):
        want = across + float(p * TILE)
        upto, here = zero, zero
        for q in range(groups):
            upto = upto + jnp.where(tall_spot[q] <= want, 1.0, 0.0)
            here = here + jnp.where(tall_spot[q] == want, 1.0, 0.0)
        upto = jnp.sum(upto, axis=0, keepdims=True)
        here = jnp.sum(here, axis=0, keepdims=True)
        last_out[:, pl.ds(p * TILE, TILE)] = jnp.where(here > 0.0, upto - 1.0, float(slots)).astype(jnp.int32)


def layer_kernel(dom_size, rep_size, *refs):
    chips = dom_size // 2
    (
        count_ref, x_hbm, weight_hbm, cot_hbm, row_hbm, col_hbm, tiles_hbm, out_ref, gp_ref, gw_ref,
        source, raw, scan, weight_ref, cot_ref, row_v, col_v, order_v, place_v, last_v, order, place, last,
        part_send, part_recv, held, grads, back, pair, up_send, up_recv, down_send, down_recv,
        gw1_send, gw1_recv, gw2_send, gw2_recv, gw3_recv,
        raw_sem, small_sem, table_sem, lift_ssem, lift_rsem, sink_ssem, sink_rsem, share_ssem, share_rsem,
        part_ssem, part_rsem, grad_ssem, grad_rsem, pair_ssem, pair_rsem, up_ssem, up_rsem, down_ssem, down_rsem,
        gw1_ssem, gw1_rsem, gw2_ssem, gw2_rsem, gw3_ssem, gw3_rsem,
    ) = refs
    rows, width = cot_ref.shape
    slots = raw.shape[0]
    blocks = rows // TILE
    col_blocks = dom_size * blocks
    me_d, me_r = lax.axis_index("dom"), lax.axis_index("rep")
    chip, core = me_d // 2, lax.rem(me_d, 2)
    partner = chip * 2 + 1 - core
    share = width // dom_size

    def dom_peer(i):
        return lax.rem(me_d + i, dom_size)

    def rep_peer(i):
        return lax.rem(me_r + i, rep_size)

    barrier = pltpu.get_barrier_semaphore()
    for i in range(1, dom_size):
        pl.semaphore_signal(barrier, inc=1, device_id=(dom_peer(i), me_r), device_id_type=MESH)
    for i in range(1, rep_size):
        pl.semaphore_signal(barrier, inc=1, device_id=(me_d, rep_peer(i)), device_id_type=MESH)

    small = [
        pltpu.make_async_copy(row_hbm, row_v, small_sem.at[0]),
        pltpu.make_async_copy(col_hbm, col_v, small_sem.at[1]),
        pltpu.make_async_copy(
            x_hbm, source.at[pl.ds(pl.multiple_of(me_d * rows, rows), rows)], small_sem.at[2]
        ),
        pltpu.make_async_copy(weight_hbm, weight_ref, small_sem.at[3]),
        pltpu.make_async_copy(cot_hbm, cot_ref, small_sem.at[4]),
    ]
    for copy in small:
        copy.start()
    per_load = slots // LOADS
    loads = [
        pltpu.make_async_copy(
            tiles_hbm.at[pl.ds(c * per_load, per_load)], raw.at[pl.ds(c * per_load, per_load)], raw_sem.at[c]
        )
        for c in range(LOADS)
    ]
    for copy in loads:
        copy.start()

    step = rows // SUB

    def lines_of(s, side, b):
        return pl.ds(pl.multiple_of((s * 2 + side) * rows + b * step, step), step)

    def hop(n, b, s, to, ssem, rsem):
        here = x_hbm.at[pl.ds(b * step, step)] if n == 0 else source.at[lines_of(s, core, b)]
        return pltpu.make_async_remote_copy(
            src_ref=here, dst_ref=source.at[lines_of(s, core, b)],
            send_sem=ssem.at[n * SUB + b], recv_sem=rsem.at[n * SUB + b],
            device_id=(to * 2 + core, me_r), device_id_type=MESH,
        )

    def lift(n, b):
        return hop(n, b, chip - n, chip + 1, lift_ssem, lift_rsem)

    def sink(n, b):
        return hop(n, b, chip + n, chip - 1, sink_ssem, sink_rsem)

    def pass_on(s, b, own):
        here = x_hbm.at[pl.ds(b * step, step)] if own else source.at[lines_of(s, core, b)]
        return pltpu.make_async_remote_copy(
            src_ref=here, dst_ref=source.at[lines_of(s, core, b)],
            send_sem=share_ssem.at[s * SUB + b], recv_sem=share_rsem.at[s * SUB + b],
            device_id=(partner, me_r), device_id_type=MESH,
        )

    pl.semaphore_wait(barrier, dom_size + rep_size - 2)
    for b in range(SUB):

        @pl.when(chip < chips - 1)
        def _():
            lift(0, b).start()

        @pl.when(chip > 0)
        def _():
            sink(0, b).start()

    for b in range(SUB):
        pass_on(chip, b, True).start()

    def relay_source(n, b):
        @pl.when(chip - 1 - n >= 0)
        def _():
            lift(n, b).wait_recv()
            if n + 1 < chips - 1:

                @pl.when(chip < chips - 1)
                def _():
                    lift(n + 1, b).start()

            pass_on(chip - 1 - n, b, False).start()

        @pl.when(chip + 1 + n < chips)
        def _():
            sink(n, b).wait_recv()
            if n + 1 < chips - 1:

                @pl.when(chip > 0)
                def _():
                    sink(n + 1, b).start()

            pass_on(chip + 1 + n, b, False).start()

    small[0].wait()
    small[1].wait()
    order_tiles(count_ref[0], row_v[...], col_v[...], col_blocks, order_v, place_v, last_v)
    tables = [
        pltpu.make_async_copy(order_v, order, table_sem.at[0]),
        pltpu.make_async_copy(place_v, place, table_sem.at[1]),
        pltpu.make_async_copy(last_v, last, table_sem.at[2]),
    ]
    for copy in tables:
        copy.start()
    events = [(n, b) for n in range(chips - 1) for b in range(SUB)]
    relay_source(*events[0])
    scan[slots] = jnp.zeros((TILE, TILE), jnp.bfloat16)
    for copy in tables + loads + small[2:]:
        copy.wait()

    def merge(k, running):
        tile = raw[jnp.clip(order[0, k], 0, slots - 1)].astype(jnp.float32)
        more = place[0, k] == place[0, jnp.maximum(k - 1, 0)]
        running = jnp.where(more, running + tile, tile)
        scan[k] = running.astype(jnp.bfloat16)
        return running

    running = jnp.zeros((TILE, TILE), jnp.float32)
    early = [e for e in events[1:] if e[0] < chips - 2]
    spans = len(early) + 1
    ends = [slots * i // spans for i in range(spans + 1)]
    for i in range(spans):
        running = lax.fori_loop(ends[i], ends[i + 1], merge, running, unroll=2)
        if i < len(early):
            relay_source(*early[i])

    def at_place(spot):
        return scan[jnp.clip(last[0, spot], 0, slots)]

    def tile_rows(first, count, left, across):
        return jnp.concatenate(
            [
                jnp.concatenate(
                    [at_place((first + i) * col_blocks + left + j) for j in range(across)], axis=1
                )
                for i in range(count)
            ],
            axis=0,
        )

    def part_copy(t):
        return pltpu.make_async_remote_copy(
            src_ref=part_send.at[t], dst_ref=part_recv.at[t],
            send_sem=part_ssem.at[t], recv_sem=part_rsem.at[t],
            device_id=(me_d, rep_peer(t + 1)), device_id_type=MESH,
        )

    half = rows // 2

    def nearest(j):
        low = jnp.minimum(chip, chips - 1 - chip)
        n = (j - 1) // 2
        both = chip + (n + 1) * (2 * ((j - 1) % 2) - 1)
        up = jnp.where(chip < chips - 1 - chip, j, chips - 1 - j)
        return jnp.where(j <= 2 * low, both, up) if j else chip

    def forward(j):
        s = nearest(j)
        for b in range(SUB):
            pass_on(s, b, False).wait_recv()
        final = j == chips - 1

        def one(i, carry):
            t, h = i // 2, lax.rem(i, 2)
            ahead = rep_peer(t + 1)
            lines = pl.ds(pl.multiple_of(h * half, half), half)
            lanes = pl.ds(pl.multiple_of(h * width, width), width)
            left = tile_rows(ahead * blocks + h * (blocks // 2), blocks // 2, s * 2 * blocks, 2 * blocks)
            right = source[pl.ds(pl.multiple_of(s * 2 * rows, rows), 2 * rows), :]
            total = jnp.dot(left, right, preferred_element_type=jnp.float32)
            if j > 0:
                total = total + back[t, :, lanes]
            if not final:
                back[t, :, lanes] = total
                return carry

            @pl.when(t < rep_size - 1)
            def _():
                part_send[t, lines, :] = total.astype(jnp.bfloat16)

            @pl.when(t == rep_size - 1)
            def _():
                held[lines, :] = total

            @pl.when((t < rep_size - 1) & (h == 1))
            def _():
                part_copy(t).start()

            return carry

        lax.fori_loop(0, 2 * rep_size, one, 0)

    for j in range(chips):
        if j == chips - 1:
            for b in range(SUB):
                relay_source(chips - 2, b)
        forward(j)

    for t in range(rep_size - 1):
        part_copy(t).wait_recv()

    weight = weight_ref[...]

    def finish(h, carry):
        lines = pl.ds(pl.multiple_of(h * 128, 128), 128)
        total = held[lines, :]
        for t in range(rep_size - 1):
            total = total + part_recv[t, lines, :].astype(jnp.float32)
        high = total.astype(jnp.bfloat16)
        low = (total - high.astype(jnp.float32)).astype(jnp.bfloat16)
        summed = jnp.dot(high, weight, preferred_element_type=jnp.float32) + jnp.dot(
            low, weight, preferred_element_type=jnp.float32
        )
        sig = jax.nn.sigmoid(summed)
        out_ref[lines, :] = (summed * sig).astype(jnp.bfloat16)
        slope = sig * (1.0 + summed * (1.0 - sig))
        grad = (cot_ref[lines, :].astype(jnp.float32) * slope).astype(jnp.bfloat16)
        grads[0, lines, :] = grad
        held[lines, :] = total
        return carry

    lax.fori_loop(0, rows // 128, finish, 0)

    def grad_copy(u):
        return pltpu.make_async_remote_copy(
            src_ref=grads.at[0], dst_ref=grads.at[u],
            send_sem=grad_ssem.at[u], recv_sem=grad_rsem.at[u],
            device_id=(me_d, rep_peer(u)), device_id_type=MESH,
        )

    for u in range(1, rep_size):
        grad_copy(u).start()

    total = held[...]
    high = total.astype(jnp.bfloat16)
    low = (total - high.astype(jnp.float32)).astype(jnp.bfloat16)
    own_grad = grads[0]
    over_rows = (((0,), (0,)), ((), ()))
    own_term = lax.dot_general(high, own_grad, over_rows, preferred_element_type=jnp.float32)
    own_term = own_term + lax.dot_general(low, own_grad, over_rows, preferred_element_type=jnp.float32)
    gw2_send[...] = own_term
    gw1_send[...] = own_term.astype(jnp.bfloat16).reshape(dom_size, share, width)

    def gw1_copy(i):
        return pltpu.make_async_remote_copy(
            src_ref=gw1_send.at[dom_peer(i)], dst_ref=gw1_recv.at[i],
            send_sem=gw1_ssem.at[i], recv_sem=gw1_rsem.at[i],
            device_id=(dom_peer(i), me_r), device_id_type=MESH,
        )

    for i in range(1, dom_size):
        gw1_copy(i).start()

    def gw2_copy(i):
        return pltpu.make_async_remote_copy(
            src_ref=gw2_recv.at[me_r], dst_ref=gw2_recv.at[me_r],
            send_sem=gw2_ssem.at[i], recv_sem=gw2_rsem.at[i],
            device_id=(me_d, rep_peer(i)), device_id_type=MESH,
        )

    def gw3_copy(i):
        return pltpu.make_async_remote_copy(
            src_ref=gw3_recv.at[me_d], dst_ref=gw3_recv.at[me_d],
            send_sem=gw3_ssem.at[i], recv_sem=gw3_rsem.at[i],
            device_id=(dom_peer(i), me_r), device_id_type=MESH,
        )

    def weight_second():
        for i in range(1, dom_size):
            gw1_copy(i).wait_recv()
        mine = gw2_send[pl.ds(pl.multiple_of(me_d * share, share), share), :]
        for i in range(1, dom_size):
            mine = mine + gw1_recv[i].astype(jnp.float32)
        gw2_recv[me_r] = mine
        for i in range(1, rep_size):
            gw2_copy(i).start()

    def weight_third():
        for i in range(1, rep_size):
            gw2_copy(i).wait_recv()
        mine = gw2_recv[0]
        for i in range(1, rep_size):
            mine = mine + gw2_recv[i]
        gw3_recv[me_d] = mine.astype(jnp.bfloat16)
        for i in range(1, dom_size):
            gw3_copy(i).start()

    def back_step(u, flipped, group, d):
        right = tile_rows(group * blocks, blocks, d * blocks, blocks)
        product = jnp.dot(flipped, right, preferred_element_type=jnp.float32)

        @pl.when(u == 0)
        def _():
            back[d] = product

        @pl.when(u > 0)
        def _():
            back[d] = back[d] + product

    part = width // SPLIT

    def turn(j):
        odd = lax.rem(j, 2)
        return (1 - odd) * (chips - 1 - j // 2) + odd * (j // 2)

    def pair_copy(j):
        there = turn(j)
        return pltpu.make_async_remote_copy(
            src_ref=back.at[there * 2 + 1 - core], dst_ref=pair.at[there],
            send_sem=pair_ssem.at[j], recv_sem=pair_rsem.at[j],
            device_id=(partner, me_r), device_id_type=MESH,
        )

    def up_copy(q):
        return pltpu.make_async_remote_copy(
            src_ref=up_send.at[q], dst_ref=up_recv.at[q],
            send_sem=up_ssem.at[q], recv_sem=up_rsem.at[q],
            device_id=((chip + 1) * 2 + core, me_r), device_id_type=MESH,
        )

    def down_copy(q):
        return pltpu.make_async_remote_copy(
            src_ref=down_send.at[q], dst_ref=down_recv.at[q],
            send_sem=down_ssem.at[q], recv_sem=down_rsem.at[q],
            device_id=((chip - 1) * 2 + core, me_r), device_id_type=MESH,
        )

    def own_part(there, q):
        lines = pl.ds(pl.multiple_of(lax.rem(q, SPLIT) * part, part), part)
        return back[there * 2 + core, lines, :]

    def relay(tick):
        q_up = tick - chip
        q_down = tick - (chips - 1 - chip)

        @pl.when((chip > 0) & (q_up >= 0) & (q_up < SPLIT * (chips - 1 - chip)))
        def _():
            up_copy(q_up).wait_recv()
            up_send[q_up] = (
                own_part(chips - 1 - q_up // SPLIT, q_up) + up_recv[q_up].astype(jnp.float32)
            ).astype(jnp.bfloat16)
            up_copy(q_up).start()

        @pl.when((chip < chips - 1) & (q_down >= 0) & (q_down < SPLIT * chip))
        def _():
            down_copy(q_down).wait_recv()
            down_send[q_down] = (
                own_part(q_down // SPLIT, q_down) + down_recv[q_down].astype(jnp.float32)
            ).astype(jnp.bfloat16)
            down_copy(q_down).start()

    for u in range(rep_size):
        slot = rep_peer(rep_size - u)
        if u > 0:
            grad_copy(u).wait_recv()
        flipped = jnp.transpose(grads[u].astype(jnp.float32)).astype(jnp.bfloat16)
        if u < rep_size - 1:
            lax.fori_loop(0, dom_size, lambda d, c: (back_step(u, flipped, slot, d), c)[1], 0)
            if u == 1:
                weight_second()
            if u == 2:
                weight_third()
        else:

            def toward(j, carry):
                back_step(u, flipped, slot, turn(j) * 2 + 1 - core)
                pair_copy(j).start()
                return carry

            def keep(j, carry):
                there = turn(j)
                back_step(u, flipped, slot, there * 2 + core)
                pair_copy(j).wait_recv()
                back[there * 2 + core] = back[there * 2 + core] + pair[there]

                @pl.when((chip == 0) & (there > 0))
                def _():
                    for h in range(SPLIT):
                        q = (chips - 1 - there) * SPLIT + h
                        up_send[q] = own_part(there, q).astype(jnp.bfloat16)
                        up_copy(q).start()

                @pl.when((chip == chips - 1) & (there < chips - 1))
                def _():
                    for h in range(SPLIT):
                        q = there * SPLIT + h
                        down_send[q] = own_part(there, q).astype(jnp.bfloat16)
                        down_copy(q).start()

                return carry

            lax.fori_loop(0, chips, toward, 0)
            lax.fori_loop(0, chips, keep, 0)

    lax.fori_loop(1, SPLIT * (chips - 2) + 1, lambda tick, c: (relay(tick), c)[1], 0)

    for h in range(SPLIT):
        lines = pl.ds(h * part, part)

        @pl.when(chip > 0)
        def _():
            q = (chips - 1 - chip) * SPLIT + h
            up_copy(q).wait_recv()
            back[me_d, lines, :] = back[me_d, lines, :] + up_recv[q].astype(jnp.float32)

        @pl.when(chip < chips - 1)
        def _():
            q = chip * SPLIT + h
            down_copy(q).wait_recv()
            back[me_d, lines, :] = back[me_d, lines, :] + down_recv[q].astype(jnp.float32)

        gp_ref[lines, :] = back[me_d, lines, :].astype(jnp.bfloat16)

    for i in range(1, dom_size):
        gw3_copy(i).wait_recv()
    gw_ref[...] = gw3_recv[...].reshape(width, width)
    for t in range(rep_size - 1):
        part_copy(t).wait_send()
    for u in range(1, rep_size):
        grad_copy(u).wait_send()
        gw2_copy(u).wait_send()
    for i in range(1, dom_size):
        gw1_copy(i).wait_send()
        gw3_copy(i).wait_send()
    for j in range(chips):
        pair_copy(j).wait_send()

    def sent(q, carry):
        @pl.when((chip < chips - 1) & (q < SPLIT * (chips - 1 - chip)))
        def _():
            up_copy(q).wait_send()

        @pl.when((chip > 0) & (q < SPLIT * chip))
        def _():
            down_copy(q).wait_send()

        return carry

    lax.fori_loop(0, SPLIT * (chips - 1), sent, 0)

    for n in range(chips - 1):
        for b in range(SUB):

            @pl.when((chip < chips - 1) & (chip - n >= 0))
            def _():
                lift(n, b).wait_send()

            @pl.when((chip > 0) & (chip + n < chips))
            def _():
                sink(n, b).wait_send()

    for s in range(chips):
        for b in range(SUB):
            pass_on(s, b, False).wait_send()


def finish_kernel(raw_ref, gp_ref, gw_in_ref, weight_ref, out_ref, gf_ref, gw_ref):
    out_ref[...] = raw_ref[...]
    gw_ref[...] = gw_in_ref[...].astype(jnp.float32)
    grad_projected = jnp.transpose(gp_ref[...])
    gf_ref[...] = lax.dot_general(
        grad_projected, weight_ref[...], (((1,), (1,)), ((), ())), preferred_element_type=jnp.float32
    ).astype(jnp.bfloat16)


def finish(raw, grad_projected, grad_weight, weight):
    here = pl.BlockSpec(memory_space=pltpu.VMEM)
    return pl.pallas_call(
        finish_kernel,
        out_shape=(
            jax.ShapeDtypeStruct(raw.shape, jnp.bfloat16),
            jax.ShapeDtypeStruct(raw.shape, jnp.bfloat16),
            jax.ShapeDtypeStruct(grad_weight.shape, jnp.float32),
        ),
        in_specs=[here] * 4,
        out_specs=(here, here, here),
        name="finish",
        compiler_params=pltpu.CompilerParams(vmem_limit_bytes=16 * 2**20),
    )(raw, grad_projected, grad_weight, weight)


def room(scratch, extra):
    total = 0
    for item in scratch:
        if getattr(item, "memory_space", None) == pltpu.VMEM:
            size = jnp.dtype(item.dtype).itemsize
            for length in item.shape:
                size *= length
            total += size
    return total + extra


def run_layer(count, features, weight, cotangent, row_index, col_index, tiles, dom_size, rep_size):
    rows, width = cotangent.shape
    chips = dom_size // 2
    share = width // dom_size
    slots = tiles.shape[0]
    places = dom_size * rep_size * (rows // TILE) ** 2
    assert rows == 2 * width and rep_size <= dom_size
    here = pl.BlockSpec(memory_space=pltpu.VMEM)
    away = pl.BlockSpec(memory_space=pl.ANY)
    sems = lambda count: pltpu.SemaphoreType.DMA((count,))
    half, full, whole = jnp.bfloat16, jnp.float32, jnp.int32
    hops = SPLIT * (chips - 1)
    walks = SUB * (chips - 1)
    scratch = [
        pltpu.VMEM((dom_size * rows, width), half),
        pltpu.VMEM((slots, TILE, TILE), half),
        pltpu.VMEM((slots + 1, TILE, TILE), half),
        pltpu.VMEM((width, width), half),
        pltpu.VMEM((rows, width), half),
        pltpu.VMEM((1, slots), whole),
        pltpu.VMEM((1, slots), whole),
        pltpu.VMEM((1, slots), whole),
        pltpu.VMEM((1, slots), whole),
        pltpu.VMEM((1, places), whole),
        pltpu.SMEM((1, slots), whole),
        pltpu.SMEM((1, slots), whole),
        pltpu.SMEM((1, places), whole),
        pltpu.VMEM((rep_size - 1, rows, width), half),
        pltpu.VMEM((rep_size - 1, rows, width), half),
        pltpu.VMEM((rows, width), full),
        pltpu.VMEM((rep_size, rows, width), half),
        pltpu.VMEM((dom_size, width, rows), full),
        pltpu.VMEM((chips, width, rows), full),
        pltpu.VMEM((hops, width // SPLIT, rows), half),
        pltpu.VMEM((hops, width // SPLIT, rows), half),
        pltpu.VMEM((hops, width // SPLIT, rows), half),
        pltpu.VMEM((hops, width // SPLIT, rows), half),
        pltpu.VMEM((dom_size, share, width), half),
        pltpu.VMEM((dom_size, share, width), half),
        pltpu.VMEM((width, width), full),
        pltpu.VMEM((rep_size, share, width), full),
        pltpu.VMEM((dom_size, share, width), half),
        sems(LOADS), sems(5), sems(3), sems(walks), sems(walks), sems(walks), sems(walks),
        sems(SUB * chips), sems(SUB * chips),
        sems(rep_size), sems(rep_size), sems(rep_size), sems(rep_size),
        sems(chips), sems(chips), sems(hops), sems(hops), sems(hops), sems(hops),
        sems(dom_size), sems(dom_size), sems(rep_size), sems(rep_size),
        sems(dom_size), sems(dom_size),
    ]
    return pl.pallas_call(
        functools.partial(layer_kernel, dom_size, rep_size),
        out_shape=(
            jax.ShapeDtypeStruct((rows, width), half),
            jax.ShapeDtypeStruct((width, rows), half),
            jax.ShapeDtypeStruct((width, width), half),
        ),
        in_specs=[pl.BlockSpec(memory_space=pltpu.SMEM)] + [away] * 6,
        out_specs=(here, here, here),
        scratch_shapes=scratch,
        name="layer",
        compiler_params=pltpu.CompilerParams(
            collective_id=0, has_side_effects=True, vmem_limit_bytes=min(room(scratch, 6 * 2**20), 67043328)
        ),
    )(count, features, weight, cotangent, row_index, col_index, tiles)


def body(node_features, weight, cotangent, tile_row, tile_col, tile_values, tile_count):
    dom_size = lax.axis_size("dom")
    rep_size = lax.axis_size("rep")
    slots = tile_row.shape[2]
    raw, grad_projected, grad_weight = run_layer(
        tile_count.reshape(1),
        node_features,
        weight,
        cotangent,
        tile_row.reshape(1, slots),
        tile_col.reshape(1, slots),
        tile_values.reshape(slots, TILE, TILE),
        dom_size,
        rep_size,
    )
    return tuple(finish(raw, grad_projected, grad_weight, weight))


def solution(mesh):
    placed = (
        P(("dom", "rep"), None),
        P(),
        P(("dom", "rep"), None),
        P("dom", "rep", None),
        P("dom", "rep", None),
        P("dom", "rep", None, None, None),
        P("dom", "rep"),
    )
    return jax.shard_map(
        body,
        mesh=mesh,
        in_specs=placed,
        out_specs=(P(("dom", "rep"), None), P(("dom", "rep"), None), P()),
        check_vma=False,
    )
```

```python
import functools

import jax
import jax.numpy as jnp
from jax import lax
from jax.experimental import pallas as pl
from jax.experimental.pallas import tpu as pltpu
from jax.sharding import PartitionSpec as P

LOADS = 8
SUB = 2
SPLIT = 4
HALVES = 2
TILE = 128
MESH = pl.DeviceIdType.MESH


def order_tiles(count, row, col, col_blocks, order_out, place_out, last_out):
    slots, places = order_out.shape[1], last_out.shape[1]
    square = (TILE, TILE)
    lane = lax.broadcasted_iota(jnp.int32, (1, slots), 1)
    spot = jnp.where(lane < count, row * col_blocks + col, places)
    key = (spot * slots + lane).astype(jnp.float32)
    spot = spot.astype(jnp.float32)
    across = lax.broadcasted_iota(jnp.int32, square, 1).astype(jnp.float32)
    down = lax.broadcasted_iota(jnp.int32, square, 0).astype(jnp.float32)
    ones = jnp.ones(square, jnp.bfloat16)
    groups = slots // TILE
    zero = jnp.zeros(square, jnp.float32)

    def wide(values, q):
        return jnp.broadcast_to(values[:, q * TILE : (q + 1) * TILE], square)

    tall_spot, rank = [], []
    for q in range(groups):
        tall_key = jnp.transpose(wide(key, q))
        tall_spot.append(jnp.transpose(wide(spot, q)))
        ahead = zero
        for j in range(groups):
            ahead = ahead + jnp.where(wide(key, j) < tall_key, 1.0, 0.0)
        rank.append(jnp.dot(ahead.astype(jnp.bfloat16), ones, preferred_element_type=jnp.float32))
    for r in range(groups):
        want = across + float(r * TILE)
        slot, place = zero, zero
        for q in range(groups):
            hit = rank[q] == want
            slot = slot + jnp.where(hit, down + float(q * TILE), 0.0)
            place = place + jnp.where(hit, tall_spot[q], 0.0)
        order_out[:, pl.ds(r * TILE, TILE)] = jnp.sum(slot, axis=0, keepdims=True).astype(jnp.int32)
        place_out[:, pl.ds(r * TILE, TILE)] = jnp.sum(place, axis=0, keepdims=True).astype(jnp.int32)
    for p in range(places // TILE):
        want = across + float(p * TILE)
        upto, here = zero, zero
        for q in range(groups):
            upto = upto + jnp.where(tall_spot[q] <= want, 1.0, 0.0)
            here = here + jnp.where(tall_spot[q] == want, 1.0, 0.0)
        upto = jnp.sum(upto, axis=0, keepdims=True)
        here = jnp.sum(here, axis=0, keepdims=True)
        last_out[:, pl.ds(p * TILE, TILE)] = jnp.where(here > 0.0, upto - 1.0, float(slots)).astype(jnp.int32)


def layer_kernel(dom_size, rep_size, *refs):
    chips = dom_size // 2
    (
        count_ref, x_hbm, weight_hbm, cot_hbm, row_hbm, col_hbm, tiles_hbm, out_ref, gp_ref, gw_ref,
        source, raw, scan, weight_ref, cot_ref, row_v, col_v, order_v, place_v, last_v, order, place, last,
        near_send, near_recv, far_send, far_recv, held, grads, back, pair, up_send, up_recv, down_send, down_recv,
        gw1_send, gw1_recv, gw2_send, gw2_recv, gw3_recv,
        raw_sem, small_sem, table_sem, lift_ssem, lift_rsem, sink_ssem, sink_rsem, share_ssem, share_rsem,
        near_ssem, near_rsem, far_ssem, far_rsem, grad_ssem, grad_rsem, pair_ssem, pair_rsem, up_ssem, up_rsem, down_ssem, down_rsem,
        gw1_ssem, gw1_rsem, gw2_ssem, gw2_rsem, gw3_ssem, gw3_rsem,
    ) = refs
    rows, width = cot_ref.shape
    slots = raw.shape[0]
    blocks = rows // TILE
    col_blocks = dom_size * blocks
    me_d, me_r = lax.axis_index("dom"), lax.axis_index("rep")
    chip, core = me_d // 2, lax.rem(me_d, 2)
    partner = chip * 2 + 1 - core
    share = width // dom_size

    def dom_peer(i):
        return lax.rem(me_d + i, dom_size)

    def rep_peer(i):
        return lax.rem(me_r + i, rep_size)

    barrier = pltpu.get_barrier_semaphore()
    for i in range(1, dom_size):
        pl.semaphore_signal(barrier, inc=1, device_id=(dom_peer(i), me_r), device_id_type=MESH)
    for i in range(1, rep_size):
        pl.semaphore_signal(barrier, inc=1, device_id=(me_d, rep_peer(i)), device_id_type=MESH)

    small = [
        pltpu.make_async_copy(row_hbm, row_v, small_sem.at[0]),
        pltpu.make_async_copy(col_hbm, col_v, small_sem.at[1]),
        pltpu.make_async_copy(
            x_hbm, source.at[pl.ds(pl.multiple_of(me_d * rows, rows), rows)], small_sem.at[2]
        ),
        pltpu.make_async_copy(weight_hbm, weight_ref, small_sem.at[3]),
        pltpu.make_async_copy(cot_hbm, cot_ref, small_sem.at[4]),
    ]
    for copy in small:
        copy.start()
    per_load = slots // LOADS
    loads = [
        pltpu.make_async_copy(
            tiles_hbm.at[pl.ds(c * per_load, per_load)], raw.at[pl.ds(c * per_load, per_load)], raw_sem.at[c]
        )
        for c in range(LOADS)
    ]
    for copy in loads:
        copy.start()

    step = rows // SUB

    def lines_of(s, side, b):
        return pl.ds(pl.multiple_of((s * 2 + side) * rows + b * step, step), step)

    def hop(n, b, s, to, ssem, rsem):
        here = x_hbm.at[pl.ds(b * step, step)] if n == 0 else source.at[lines_of(s, core, b)]
        return pltpu.make_async_remote_copy(
            src_ref=here, dst_ref=source.at[lines_of(s, core, b)],
            send_sem=ssem.at[n * SUB + b], recv_sem=rsem.at[n * SUB + b],
            device_id=(to * 2 + core, me_r), device_id_type=MESH,
        )

    def lift(n, b):
        return hop(n, b, chip - n, chip + 1, lift_ssem, lift_rsem)

    def sink(n, b):
        return hop(n, b, chip + n, chip - 1, sink_ssem, sink_rsem)

    def pass_on(s, b, own):
        here = x_hbm.at[pl.ds(b * step, step)] if own else source.at[lines_of(s, core, b)]
        return pltpu.make_async_remote_copy(
            src_ref=here, dst_ref=source.at[lines_of(s, core, b)],
            send_sem=share_ssem.at[s * SUB + b], recv_sem=share_rsem.at[s * SUB + b],
            device_id=(partner, me_r), device_id_type=MESH,
        )

    pl.semaphore_wait(barrier, dom_size + rep_size - 2)
    for b in range(SUB):

        @pl.when(chip < chips - 1)
        def _():
            lift(0, b).start()

        @pl.when(chip > 0)
        def _():
            sink(0, b).start()

    for b in range(SUB):
        pass_on(chip, b, True).start()

    def relay_source(n, b):
        @pl.when(chip - 1 - n >= 0)
        def _():
            lift(n, b).wait_recv()
            if n + 1 < chips - 1:

                @pl.when(chip < chips - 1)
                def _():
                    lift(n + 1, b).start()

            pass_on(chip - 1 - n, b, False).start()

        @pl.when(chip + 1 + n < chips)
        def _():
            sink(n, b).wait_recv()
            if n + 1 < chips - 1:

                @pl.when(chip > 0)
                def _():
                    sink(n + 1, b).start()

            pass_on(chip + 1 + n, b, False).start()

    small[0].wait()
    small[1].wait()
    order_tiles(count_ref[0], row_v[...], col_v[...], col_blocks, order_v, place_v, last_v)
    tables = [
        pltpu.make_async_copy(order_v, order, table_sem.at[0]),
        pltpu.make_async_copy(place_v, place, table_sem.at[1]),
        pltpu.make_async_copy(last_v, last, table_sem.at[2]),
    ]
    for copy in tables:
        copy.start()
    events = [(n, b) for n in range(chips - 1) for b in range(SUB)]
    relay_source(*events[0])
    scan[slots] = jnp.zeros((TILE, TILE), jnp.bfloat16)
    for copy in tables + loads + small[2:]:
        copy.wait()
    if len(events) > 1:
        relay_source(*events[1])

    def merge(k, running):
        tile = raw[jnp.clip(order[0, k], 0, slots - 1)].astype(jnp.float32)
        more = place[0, k] == place[0, jnp.maximum(k - 1, 0)]
        running = jnp.where(more, running + tile, tile)
        scan[k] = running.astype(jnp.bfloat16)
        return running

    running = jnp.zeros((TILE, TILE), jnp.float32)
    early = [e for e in events[2:] if e[0] < chips - 2]
    spans = max(len(early), 1)
    ends = [slots * i // spans for i in range(spans + 1)]
    for i in range(spans):
        running = lax.fori_loop(ends[i], ends[i + 1], merge, running, unroll=2)
        if i < len(early):
            relay_source(*early[i])

    def at_place(spot):
        return scan[jnp.clip(last[0, spot], 0, slots)]

    def tile_rows(first, count, left, across):
        return jnp.concatenate(
            [
                jnp.concatenate(
                    [at_place((first + i) * col_blocks + left + j) for j in range(across)], axis=1
                )
                for i in range(count)
            ],
            axis=0,
        )

    outer_size = rep_size // 2
    outer, inner = me_r // 2, lax.rem(me_r, 2)

    def outer_peer(i):
        return lax.rem(outer + i, outer_size)

    def near_copy(i):
        return pltpu.make_async_remote_copy(
            src_ref=near_send.at[i], dst_ref=near_recv.at[i],
            send_sem=near_ssem.at[i], recv_sem=near_rsem.at[i],
            device_id=(me_d, outer * 2 + 1 - inner), device_id_type=MESH,
        )

    def far_copy(i, k):
        return pltpu.make_async_remote_copy(
            src_ref=far_send.at[i - 1, k], dst_ref=far_recv.at[i - 1, k],
            send_sem=far_ssem.at[(i - 1) * 3 + k], recv_sem=far_rsem.at[(i - 1) * 3 + k],
            device_id=(me_d, outer_peer(i) * 2 + inner), device_id_type=MESH,
        )

    half = rows // 2

    def nearest(j):
        low = jnp.minimum(chip, chips - 1 - chip)
        n = (j - 1) // 2
        both = chip + (n + 1) * (2 * ((j - 1) % 2) - 1)
        up = jnp.where(chip < chips - 1 - chip, j, chips - 1 - j)
        return jnp.where(j <= 2 * low, both, up) if j else chip

    def forward(j):
        s = nearest(j)
        for b in range(SUB):
            pass_on(s, b, False).wait_recv()
        final = j == chips - 1

        def one(t, carry):
            i = lax.rem(t // 2 + 1, outer_size)
            side = lax.rem(t, 2)
            ahead = outer_peer(i) * 2 + (1 - side) * (1 - inner) + side * inner
            left = tile_rows(ahead * blocks, blocks, s * 2 * blocks, 2 * blocks)
            right = source[pl.ds(pl.multiple_of(s * 2 * rows, rows), 2 * rows), :]
            total = jnp.dot(left, right, preferred_element_type=jnp.float32)
            if j > 0:
                total = total + jnp.concatenate([back[t, :, :width], back[t, :, width:]], axis=0)
            if not final:
                back[t, :, :width] = total[:half]
                back[t, :, width:] = total[half:]
                return carry

            back[t, :, :width] = total[:half]
            back[t, :, width:] = total[half:]

            @pl.when(side == 0)
            def _():
                near_send[i] = total[:half].astype(jnp.bfloat16)
                near_copy(i).start()

            @pl.when(i > 0)
            def _():
                far_send[i - 1, side] = total[half:].astype(jnp.bfloat16)
                far_copy(i, side).start()

            return carry

        lax.fori_loop(0, rep_size, one, 0)

    for j in range(chips):
        if j == chips - 1:
            for b in range(SUB):
                relay_source(chips - 2, b)
        forward(j)

    for i in range(1, outer_size):
        near_copy(i).wait_recv()
        far_send[i - 1, 2] = (
            back[2 * i - 1, :, :width] + near_recv[i].astype(jnp.float32)
        ).astype(jnp.bfloat16)
        far_copy(i, 2).start()
    for i in range(1, outer_size):
        far_copy(i, 0).wait_recv()
    beside = back[rep_size - 2, :, width:]
    for i in range(1, outer_size):
        beside = beside + far_recv[i - 1, 0].astype(jnp.float32)
    near_send[outer_size] = beside.astype(jnp.bfloat16)
    near_copy(outer_size).start()
    near_copy(0).wait_recv()
    upper = back[rep_size - 1, :, :width] + near_recv[0].astype(jnp.float32)
    lower = back[rep_size - 1, :, width:]
    for i in range(1, outer_size):
        far_copy(i, 1).wait_recv()
        lower = lower + far_recv[i - 1, 1].astype(jnp.float32)
    held[:half, :] = upper
    held[half:, :] = lower
    for i in range(1, outer_size):
        far_copy(i, 2).wait_recv()
    near_copy(outer_size).wait_recv()

    weight = weight_ref[...]
    slab = width // HALVES

    def finish(h, carry):
        lines = pl.ds(pl.multiple_of(h * 128, 128), 128)
        total = held[lines, :]
        piece = pl.ds(pl.multiple_of(lax.rem(h, half // 128) * 128, 128), 128)
        late = far_recv[0, 2, piece, :].astype(jnp.float32)
        for i in range(2, outer_size):
            late = late + far_recv[i - 1, 2, piece, :].astype(jnp.float32)
        total = total + jnp.where(h < half // 128, late, near_recv[outer_size, piece, :].astype(jnp.float32))
        high = total.astype(jnp.bfloat16)
        low = (total - high.astype(jnp.float32)).astype(jnp.bfloat16)
        summed = jnp.dot(high, weight, preferred_element_type=jnp.float32) + jnp.dot(
            low, weight, preferred_element_type=jnp.float32
        )
        sig = jax.nn.sigmoid(summed)
        out_ref[lines, :] = (summed * sig).astype(jnp.bfloat16)
        slope = sig * (1.0 + summed * (1.0 - sig))
        grad = (cot_ref[lines, :].astype(jnp.float32) * slope).astype(jnp.bfloat16)
        for h in range(HALVES):
            grads[h, 0, lines, :] = grad[:, h * slab : (h + 1) * slab]
        held[lines, :] = total
        return carry

    lax.fori_loop(0, rows // 128, finish, 0)

    def grad_copy(u, h):
        return pltpu.make_async_remote_copy(
            src_ref=grads.at[h, 0], dst_ref=grads.at[h, u],
            send_sem=grad_ssem.at[h * rep_size + u], recv_sem=grad_rsem.at[h * rep_size + u],
            device_id=(me_d, rep_peer(u)), device_id_type=MESH,
        )

    for u in range(1, rep_size):
        grad_copy(u, 0).start()

    total = held[...]
    high = total.astype(jnp.bfloat16)
    low = (total - high.astype(jnp.float32)).astype(jnp.bfloat16)
    own_grad = jnp.concatenate([grads[h, 0] for h in range(HALVES)], axis=1)
    over_rows = (((0,), (0,)), ((), ()))
    own_term = lax.dot_general(high, own_grad, over_rows, preferred_element_type=jnp.float32)
    own_term = own_term + lax.dot_general(low, own_grad, over_rows, preferred_element_type=jnp.float32)
    gw2_send[...] = own_term
    gw1_send[...] = own_term.astype(jnp.bfloat16).reshape(dom_size, share, width)

    def gw1_copy(i):
        return pltpu.make_async_remote_copy(
            src_ref=gw1_send.at[dom_peer(i)], dst_ref=gw1_recv.at[i],
            send_sem=gw1_ssem.at[i], recv_sem=gw1_rsem.at[i],
            device_id=(dom_peer(i), me_r), device_id_type=MESH,
        )

    for i in range(1, dom_size):
        gw1_copy(i).start()

    def gw2_copy(i):
        return pltpu.make_async_remote_copy(
            src_ref=gw2_recv.at[me_r], dst_ref=gw2_recv.at[me_r],
            send_sem=gw2_ssem.at[i], recv_sem=gw2_rsem.at[i],
            device_id=(me_d, rep_peer(i)), device_id_type=MESH,
        )

    def gw3_copy(i):
        return pltpu.make_async_remote_copy(
            src_ref=gw3_recv.at[me_d], dst_ref=gw3_recv.at[me_d],
            send_sem=gw3_ssem.at[i], recv_sem=gw3_rsem.at[i],
            device_id=(dom_peer(i), me_r), device_id_type=MESH,
        )

    def weight_second():
        for i in range(1, dom_size):
            gw1_copy(i).wait_recv()
        mine = gw2_send[pl.ds(pl.multiple_of(me_d * share, share), share), :]
        for i in range(1, dom_size):
            mine = mine + gw1_recv[i].astype(jnp.float32)
        gw2_recv[me_r] = mine
        for i in range(1, rep_size):
            gw2_copy(i).start()

    def weight_third():
        for i in range(1, rep_size):
            gw2_copy(i).wait_recv()
        mine = gw2_recv[0]
        for i in range(1, rep_size):
            mine = mine + gw2_recv[i]
        gw3_recv[me_d] = mine.astype(jnp.bfloat16)
        for i in range(1, dom_size):
            gw3_copy(i).start()

    part = width // SPLIT
    each = SPLIT // HALVES
    hops = each * (chips - 1)

    def slab_of(h):
        return pl.ds(h * slab, slab)

    def back_step(u, h, flipped, d):
        right = tile_rows(rep_peer(rep_size - u) * blocks, blocks, d * blocks, blocks)
        product = jnp.dot(flipped, right, preferred_element_type=jnp.float32)
        if u > 0:
            product = back[d, slab_of(h), :] + product
        back[d, slab_of(h), :] = product

    def flip(u, h):
        return jnp.transpose(grads[h, u].astype(jnp.float32)).astype(jnp.bfloat16)

    def back_all(u, h):
        if u > 0:
            grad_copy(u, h).wait_recv()
        flipped = flip(u, h)
        lax.fori_loop(0, dom_size, lambda d, c: (back_step(u, h, flipped, d), c)[1], 0)

    def turn(j):
        odd = lax.rem(j, 2)
        return (1 - odd) * (chips - 1 - j // 2) + odd * (j // 2)

    def pair_copy(j, h):
        there = turn(j)
        return pltpu.make_async_remote_copy(
            src_ref=back.at[there * 2 + 1 - core, slab_of(h)], dst_ref=pair.at[there, slab_of(h)],
            send_sem=pair_ssem.at[h * chips + j], recv_sem=pair_rsem.at[h * chips + j],
            device_id=(partner, me_r), device_id_type=MESH,
        )

    def up_copy(q, h):
        return pltpu.make_async_remote_copy(
            src_ref=up_send.at[h * hops + q], dst_ref=up_recv.at[h * hops + q],
            send_sem=up_ssem.at[h * hops + q], recv_sem=up_rsem.at[h * hops + q],
            device_id=((chip + 1) * 2 + core, me_r), device_id_type=MESH,
        )

    def down_copy(q, h):
        return pltpu.make_async_remote_copy(
            src_ref=down_send.at[h * hops + q], dst_ref=down_recv.at[h * hops + q],
            send_sem=down_ssem.at[h * hops + q], recv_sem=down_rsem.at[h * hops + q],
            device_id=((chip - 1) * 2 + core, me_r), device_id_type=MESH,
        )

    def own_part(there, q, h):
        lines = pl.ds(pl.multiple_of(h * slab + lax.rem(q, each) * part, part), part)
        return back[there * 2 + core, lines, :]

    def relay(tick, h):
        q_up = tick - chip
        q_down = tick - (chips - 1 - chip)

        @pl.when((chip > 0) & (q_up >= 0) & (q_up < each * (chips - 1 - chip)))
        def _():
            up_copy(q_up, h).wait_recv()
            up_send[h * hops + q_up] = (
                own_part(chips - 1 - q_up // each, q_up, h) + up_recv[h * hops + q_up].astype(jnp.float32)
            ).astype(jnp.bfloat16)
            up_copy(q_up, h).start()

        @pl.when((chip < chips - 1) & (q_down >= 0) & (q_down < each * chip))
        def _():
            down_copy(q_down, h).wait_recv()
            down_send[h * hops + q_down] = (
                own_part(q_down // each, q_down, h) + down_recv[h * hops + q_down].astype(jnp.float32)
            ).astype(jnp.bfloat16)
            down_copy(q_down, h).start()

    def relays(first, after, h):
        lax.fori_loop(first, after, lambda tick, c: (relay(tick, h), c)[1], 0)

    def back_last(h, between):
        u = rep_size - 1
        grad_copy(u, h).wait_recv()
        flipped = flip(u, h)

        def toward(j, carry):
            back_step(u, h, flipped, turn(j) * 2 + 1 - core)
            pair_copy(j, h).start()
            return carry

        def keep(j, carry):
            there = turn(j)
            back_step(u, h, flipped, there * 2 + core)
            pair_copy(j, h).wait_recv()
            mine = there * 2 + core
            back[mine, slab_of(h), :] = back[mine, slab_of(h), :] + pair[there, slab_of(h), :]

            @pl.when((chip == 0) & (there > 0))
            def _():
                for i in range(each):
                    q = (chips - 1 - there) * each + i
                    up_send[h * hops + q] = own_part(there, q, h).astype(jnp.bfloat16)
                    up_copy(q, h).start()

            @pl.when((chip == chips - 1) & (there < chips - 1))
            def _():
                for i in range(each):
                    q = there * each + i
                    down_send[h * hops + q] = own_part(there, q, h).astype(jnp.bfloat16)
                    down_copy(q, h).start()

            return carry

        lax.fori_loop(0, chips, toward, 0)
        between()
        lax.fori_loop(0, chips, keep, 0)

    ticks = each * (chips - 2)
    for h in range(HALVES):
        back_all(0, h)
    weight_second()
    for h in range(1, HALVES):
        for u in range(1, rep_size):
            grad_copy(u, h).start()
    for u in range(1, rep_size - 1):
        back_all(u, 0)
    back_last(0, weight_third)
    for h in range(1, HALVES):
        for u in range(1, rep_size - 1):
            back_all(u, h)
            relays(1 + ticks * (u - 1) // (rep_size - 1), 1 + ticks * u // (rep_size - 1), h - 1)
        back_last(h, lambda: relays(1 + ticks * (rep_size - 2) // (rep_size - 1), 1 + ticks, h - 1))
    relays(1, 1 + ticks, HALVES - 1)

    for h in range(HALVES):
        for i in range(each):
            lines = pl.ds(h * slab + i * part, part)

            @pl.when(chip > 0)
            def _():
                q = (chips - 1 - chip) * each + i
                up_copy(q, h).wait_recv()
                back[me_d, lines, :] = back[me_d, lines, :] + up_recv[h * hops + q].astype(jnp.float32)

            @pl.when(chip < chips - 1)
            def _():
                q = chip * each + i
                down_copy(q, h).wait_recv()
                back[me_d, lines, :] = back[me_d, lines, :] + down_recv[h * hops + q].astype(jnp.float32)

            gp_ref[lines, :] = back[me_d, lines, :].astype(jnp.bfloat16)

    for i in range(1, dom_size):
        gw3_copy(i).wait_recv()
    gw_ref[...] = gw3_recv[...].reshape(width, width)
    for i in range(outer_size + 1):
        near_copy(i).wait_send()
    for i in range(1, outer_size):
        for k in range(3):
            far_copy(i, k).wait_send()
    for u in range(1, rep_size):
        for h in range(HALVES):
            grad_copy(u, h).wait_send()
        gw2_copy(u).wait_send()
    for i in range(1, dom_size):
        gw1_copy(i).wait_send()
        gw3_copy(i).wait_send()
    for j in range(chips):
        for h in range(HALVES):
            pair_copy(j, h).wait_send()

    def sent(q, carry):
        for h in range(HALVES):

            @pl.when((chip < chips - 1) & (q < each * (chips - 1 - chip)))
            def _():
                up_copy(q, h).wait_send()

            @pl.when((chip > 0) & (q < each * chip))
            def _():
                down_copy(q, h).wait_send()

        return carry

    lax.fori_loop(0, hops, sent, 0)

    for n in range(chips - 1):
        for b in range(SUB):

            @pl.when((chip < chips - 1) & (chip - n >= 0))
            def _():
                lift(n, b).wait_send()

            @pl.when((chip > 0) & (chip + n < chips))
            def _():
                sink(n, b).wait_send()

    for s in range(chips):
        for b in range(SUB):
            pass_on(s, b, False).wait_send()


def finish_kernel(raw_ref, gp_ref, gw_in_ref, weight_ref, out_ref, gf_ref, gw_ref):
    out_ref[...] = raw_ref[...]
    gw_ref[...] = gw_in_ref[...].astype(jnp.float32)
    grad_projected = jnp.transpose(gp_ref[...])
    gf_ref[...] = lax.dot_general(
        grad_projected, weight_ref[...], (((1,), (1,)), ((), ())), preferred_element_type=jnp.float32
    ).astype(jnp.bfloat16)


def finish(raw, grad_projected, grad_weight, weight):
    here = pl.BlockSpec(memory_space=pltpu.VMEM)
    return pl.pallas_call(
        finish_kernel,
        out_shape=(
            jax.ShapeDtypeStruct(raw.shape, jnp.bfloat16),
            jax.ShapeDtypeStruct(raw.shape, jnp.bfloat16),
            jax.ShapeDtypeStruct(grad_weight.shape, jnp.float32),
        ),
        in_specs=[here] * 4,
        out_specs=(here, here, here),
        name="finish",
        compiler_params=pltpu.CompilerParams(vmem_limit_bytes=16 * 2**20),
    )(raw, grad_projected, grad_weight, weight)


def room(scratch, extra):
    total = 0
    for item in scratch:
        if getattr(item, "memory_space", None) == pltpu.VMEM:
            size = jnp.dtype(item.dtype).itemsize
            for length in item.shape:
                size *= length
            total += size
    return total + extra


def run_layer(count, features, weight, cotangent, row_index, col_index, tiles, dom_size, rep_size):
    rows, width = cotangent.shape
    chips = dom_size // 2
    share = width // dom_size
    slots = tiles.shape[0]
    places = dom_size * rep_size * (rows // TILE) ** 2
    assert rows == 2 * width and rep_size <= dom_size
    here = pl.BlockSpec(memory_space=pltpu.VMEM)
    away = pl.BlockSpec(memory_space=pltpu.HBM)
    sems = lambda count: pltpu.SemaphoreType.DMA((count,))
    half, full, whole = jnp.bfloat16, jnp.float32, jnp.int32
    hops = SPLIT * (chips - 1)
    walks = SUB * (chips - 1)
    scratch = [
        pltpu.VMEM((dom_size * rows, width), half),
        pltpu.VMEM((slots, TILE, TILE), half),
        pltpu.VMEM((slots + 1, TILE, TILE), half),
        pltpu.VMEM((width, width), half),
        pltpu.VMEM((rows, width), half),
        pltpu.VMEM((1, slots), whole),
        pltpu.VMEM((1, slots), whole),
        pltpu.VMEM((1, slots), whole),
        pltpu.VMEM((1, slots), whole),
        pltpu.VMEM((1, places), whole),
        pltpu.SMEM((1, slots), whole),
        pltpu.SMEM((1, slots), whole),
        pltpu.SMEM((1, places), whole),
        pltpu.VMEM((rep_size // 2 + 1, rows // 2, width), half),
        pltpu.VMEM((rep_size // 2 + 1, rows // 2, width), half),
        pltpu.VMEM((rep_size // 2 - 1, 3, rows // 2, width), half),
        pltpu.VMEM((rep_size // 2 - 1, 3, rows // 2, width), half),
        pltpu.VMEM((rows, width), full),
        pltpu.VMEM((HALVES, rep_size, rows, width // HALVES), half),
        pltpu.VMEM((dom_size, width, rows), full),
        pltpu.VMEM((chips, width, rows), full),
        pltpu.VMEM((hops, width // SPLIT, rows), half),
        pltpu.VMEM((hops, width // SPLIT, rows), half),
        pltpu.VMEM((hops, width // SPLIT, rows), half),
        pltpu.VMEM((hops, width // SPLIT, rows), half),
        pltpu.VMEM((dom_size, share, width), half),
        pltpu.VMEM((dom_size, share, width), half),
        pltpu.VMEM((width, width), full),
        pltpu.VMEM((rep_size, share, width), full),
        pltpu.VMEM((dom_size, share, width), half),
        sems(LOADS), sems(5), sems(3), sems(walks), sems(walks), sems(walks), sems(walks),
        sems(SUB * chips), sems(SUB * chips),
        sems(rep_size // 2 + 1), sems(rep_size // 2 + 1), sems(3 * (rep_size // 2 - 1)), sems(3 * (rep_size // 2 - 1)),
        sems(HALVES * rep_size), sems(HALVES * rep_size),
        sems(HALVES * chips), sems(HALVES * chips), sems(hops), sems(hops), sems(hops), sems(hops),
        sems(dom_size), sems(dom_size), sems(rep_size), sems(rep_size),
        sems(dom_size), sems(dom_size),
    ]
    return pl.pallas_call(
        functools.partial(layer_kernel, dom_size, rep_size),
        out_shape=(
            jax.ShapeDtypeStruct((rows, width), half),
            jax.ShapeDtypeStruct((width, rows), half),
            jax.ShapeDtypeStruct((width, width), half),
        ),
        in_specs=[pl.BlockSpec(memory_space=pltpu.SMEM)] + [away] * 6,
        out_specs=(here, here, here),
        scratch_shapes=scratch,
        name="layer",
        compiler_params=pltpu.CompilerParams(
            collective_id=0, has_side_effects=True, vmem_limit_bytes=min(room(scratch, 6 * 2**20), 67043328)
        ),
    )(count, features, weight, cotangent, row_index, col_index, tiles)


def body(node_features, weight, cotangent, tile_row, tile_col, tile_values, tile_count):
    dom_size = lax.axis_size("dom")
    rep_size = lax.axis_size("rep")
    slots = tile_row.shape[2]
    raw, grad_projected, grad_weight = run_layer(
        tile_count.reshape(1),
        node_features,
        weight,
        cotangent,
        tile_row.reshape(1, slots),
        tile_col.reshape(1, slots),
        tile_values.reshape(slots, TILE, TILE),
        dom_size,
        rep_size,
    )
    return tuple(finish(raw, grad_projected, grad_weight, weight))


def solution(mesh):
    placed = (
        P(("dom", "rep"), None),
        P(),
        P(("dom", "rep"), None),
        P("dom", "rep", None),
        P("dom", "rep", None),
        P("dom", "rep", None, None, None),
        P("dom", "rep"),
    )
    return jax.shard_map(
        body,
        mesh=mesh,
        in_specs=placed,
        out_specs=(P(("dom", "rep"), None), P(("dom", "rep"), None), P()),
        check_vma=False,
    )
```

```python
import functools

import jax
import jax.numpy as jnp
from jax import lax
from jax.experimental import pallas as pl
from jax.experimental.pallas import tpu as pltpu
from jax.sharding import PartitionSpec as P

LOADS = 8
SUB = 2
SPLIT = 2
HALVES = 2
TILE = 128
MESH = pl.DeviceIdType.MESH


def order_tiles(count, row, col, col_blocks, order_out, place_out, last_out):
    slots, places = order_out.shape[1], last_out.shape[1]
    square = (TILE, TILE)
    lane = lax.broadcasted_iota(jnp.int32, (1, slots), 1)
    spot = jnp.where(lane < count, row * col_blocks + col, places)
    key = (spot * slots + lane).astype(jnp.float32)
    spot = spot.astype(jnp.float32)
    across = lax.broadcasted_iota(jnp.int32, square, 1).astype(jnp.float32)
    down = lax.broadcasted_iota(jnp.int32, square, 0).astype(jnp.float32)
    ones = jnp.ones(square, jnp.bfloat16)
    groups = slots // TILE
    zero = jnp.zeros(square, jnp.float32)

    def wide(values, q):
        return jnp.broadcast_to(values[:, q * TILE : (q + 1) * TILE], square)

    tall_spot, rank = [], []
    for q in range(groups):
        tall_key = jnp.transpose(wide(key, q))
        tall_spot.append(jnp.transpose(wide(spot, q)))
        ahead = zero
        for j in range(groups):
            ahead = ahead + jnp.where(wide(key, j) < tall_key, 1.0, 0.0)
        rank.append(jnp.dot(ahead.astype(jnp.bfloat16), ones, preferred_element_type=jnp.float32))
    for r in range(groups):
        want = across + float(r * TILE)
        slot, place = zero, zero
        for q in range(groups):
            hit = rank[q] == want
            slot = slot + jnp.where(hit, down + float(q * TILE), 0.0)
            place = place + jnp.where(hit, tall_spot[q], 0.0)
        order_out[:, pl.ds(r * TILE, TILE)] = jnp.sum(slot, axis=0, keepdims=True).astype(jnp.int32)
        place_out[:, pl.ds(r * TILE, TILE)] = jnp.sum(place, axis=0, keepdims=True).astype(jnp.int32)
    for p in range(places // TILE):
        want = across + float(p * TILE)
        upto, here = zero, zero
        for q in range(groups):
            upto = upto + jnp.where(tall_spot[q] <= want, 1.0, 0.0)
            here = here + jnp.where(tall_spot[q] == want, 1.0, 0.0)
        upto = jnp.sum(upto, axis=0, keepdims=True)
        here = jnp.sum(here, axis=0, keepdims=True)
        last_out[:, pl.ds(p * TILE, TILE)] = jnp.where(here > 0.0, upto - 1.0, float(slots)).astype(jnp.int32)


def layer_kernel(dom_size, rep_size, *refs):
    chips = dom_size // 2
    (
        count_ref, x_hbm, weight_hbm, cot_hbm, row_hbm, col_hbm, tiles_hbm, out_ref, gp_ref, gw_ref,
        source, raw, scan, weight_ref, cot_ref, row_v, col_v, order_v, place_v, last_v, order, place, last,
        near_send, near_recv, far_send, far_recv, held, grads, back, pair, up_send, up_recv, down_send, down_recv,
        gw1_send, gw1_recv, gw2_send, gw2_recv, gw3_recv,
        raw_sem, small_sem, table_sem, lift_ssem, lift_rsem, sink_ssem, sink_rsem, share_ssem, share_rsem,
        near_ssem, near_rsem, far_ssem, far_rsem, near_gsend, near_grecv, far_gsend, far_grecv, pair_ssem, pair_rsem, up_ssem, up_rsem, down_ssem, down_rsem,
        gw1_ssem, gw1_rsem, gw2_ssem, gw2_rsem, gw3_ssem, gw3_rsem,
    ) = refs
    rows, width = cot_ref.shape
    slots = raw.shape[0]
    blocks = rows // TILE
    col_blocks = dom_size * blocks
    me_d, me_r = lax.axis_index("dom"), lax.axis_index("rep")
    chip, core = me_d // 2, lax.rem(me_d, 2)
    partner = chip * 2 + 1 - core
    share = width // dom_size

    def dom_peer(i):
        return lax.rem(me_d + i, dom_size)

    def rep_peer(i):
        return lax.rem(me_r + i, rep_size)

    barrier = pltpu.get_barrier_semaphore()
    for i in range(1, dom_size):
        pl.semaphore_signal(barrier, inc=1, device_id=(dom_peer(i), me_r), device_id_type=MESH)
    for i in range(1, rep_size):
        pl.semaphore_signal(barrier, inc=1, device_id=(me_d, rep_peer(i)), device_id_type=MESH)

    small = [
        pltpu.make_async_copy(row_hbm, row_v, small_sem.at[0]),
        pltpu.make_async_copy(col_hbm, col_v, small_sem.at[1]),
        pltpu.make_async_copy(
            x_hbm, source.at[pl.ds(pl.multiple_of(me_d * rows, rows), rows)], small_sem.at[2]
        ),
        pltpu.make_async_copy(weight_hbm, weight_ref, small_sem.at[3]),
        pltpu.make_async_copy(cot_hbm, cot_ref, small_sem.at[4]),
    ]
    for copy in small:
        copy.start()
    per_load = slots // LOADS
    loads = [
        pltpu.make_async_copy(
            tiles_hbm.at[pl.ds(c * per_load, per_load)], raw.at[pl.ds(c * per_load, per_load)], raw_sem.at[c]
        )
        for c in range(LOADS)
    ]
    for copy in loads:
        copy.start()

    step = rows // SUB

    def lines_of(s, side, b):
        return pl.ds(pl.multiple_of((s * 2 + side) * rows + b * step, step), step)

    def hop(n, b, s, to, ssem, rsem):
        here = x_hbm.at[pl.ds(b * step, step)] if n == 0 else source.at[lines_of(s, core, b)]
        return pltpu.make_async_remote_copy(
            src_ref=here, dst_ref=source.at[lines_of(s, core, b)],
            send_sem=ssem.at[n * SUB + b], recv_sem=rsem.at[n * SUB + b],
            device_id=(to * 2 + core, me_r), device_id_type=MESH,
        )

    def lift(n, b):
        return hop(n, b, chip - n, chip + 1, lift_ssem, lift_rsem)

    def sink(n, b):
        return hop(n, b, chip + n, chip - 1, sink_ssem, sink_rsem)

    def pass_on(s, b, own):
        here = x_hbm.at[pl.ds(b * step, step)] if own else source.at[lines_of(s, core, b)]
        return pltpu.make_async_remote_copy(
            src_ref=here, dst_ref=source.at[lines_of(s, core, b)],
            send_sem=share_ssem.at[s * SUB + b], recv_sem=share_rsem.at[s * SUB + b],
            device_id=(partner, me_r), device_id_type=MESH,
        )

    pl.semaphore_wait(barrier, dom_size + rep_size - 2)
    for b in range(SUB):

        @pl.when(chip < chips - 1)
        def _():
            lift(0, b).start()

        @pl.when(chip > 0)
        def _():
            sink(0, b).start()

    for b in range(SUB):
        pass_on(chip, b, True).start()

    def relay_source(n, b):
        @pl.when(chip - 1 - n >= 0)
        def _():
            lift(n, b).wait_recv()
            if n + 1 < chips - 1:

                @pl.when(chip < chips - 1)
                def _():
                    lift(n + 1, b).start()

            pass_on(chip - 1 - n, b, False).start()

        @pl.when(chip + 1 + n < chips)
        def _():
            sink(n, b).wait_recv()
            if n + 1 < chips - 1:

                @pl.when(chip > 0)
                def _():
                    sink(n + 1, b).start()

            pass_on(chip + 1 + n, b, False).start()

    small[0].wait()
    small[1].wait()
    order_tiles(count_ref[0], row_v[...], col_v[...], col_blocks, order_v, place_v, last_v)
    tables = [
        pltpu.make_async_copy(order_v, order, table_sem.at[0]),
        pltpu.make_async_copy(place_v, place, table_sem.at[1]),
        pltpu.make_async_copy(last_v, last, table_sem.at[2]),
    ]
    for copy in tables:
        copy.start()
    events = [(n, b) for n in range(chips - 1) for b in range(SUB)]
    relay_source(*events[0])
    scan[slots] = jnp.zeros((TILE, TILE), jnp.bfloat16)
    for copy in tables + loads + small[2:]:
        copy.wait()
    if len(events) > 1:
        relay_source(*events[1])

    def merge(k, running):
        tile = raw[jnp.clip(order[0, k], 0, slots - 1)].astype(jnp.float32)
        more = place[0, k] == place[0, jnp.maximum(k - 1, 0)]
        running = jnp.where(more, running + tile, tile)
        scan[k] = running.astype(jnp.bfloat16)
        return running

    running = jnp.zeros((TILE, TILE), jnp.float32)
    early = [e for e in events[2:] if e[0] < chips - 2]
    spans = max(len(early), 1)
    ends = [slots * i // spans for i in range(spans + 1)]
    for i in range(spans):
        running = lax.fori_loop(ends[i], ends[i + 1], merge, running, unroll=2)
        if i < len(early):
            relay_source(*early[i])

    def at_place(spot):
        return scan[jnp.clip(last[0, spot], 0, slots)]

    def tile_rows(first, count, left, across):
        return jnp.concatenate(
            [
                jnp.concatenate(
                    [at_place((first + i) * col_blocks + left + j) for j in range(across)], axis=1
                )
                for i in range(count)
            ],
            axis=0,
        )

    outer_size = rep_size // 2
    outer, inner = me_r // 2, lax.rem(me_r, 2)

    def outer_peer(i):
        return lax.rem(outer + i, outer_size)

    def near_copy(i):
        return pltpu.make_async_remote_copy(
            src_ref=near_send.at[i], dst_ref=near_recv.at[i],
            send_sem=near_ssem.at[i], recv_sem=near_rsem.at[i],
            device_id=(me_d, outer * 2 + 1 - inner), device_id_type=MESH,
        )

    def far_copy(i, k):
        return pltpu.make_async_remote_copy(
            src_ref=far_send.at[i - 1, k], dst_ref=far_recv.at[i - 1, k],
            send_sem=far_ssem.at[(i - 1) * 3 + k], recv_sem=far_rsem.at[(i - 1) * 3 + k],
            device_id=(me_d, outer_peer(i) * 2 + inner), device_id_type=MESH,
        )

    half = rows // 2

    def nearest(j):
        low = jnp.minimum(chip, chips - 1 - chip)
        n = (j - 1) // 2
        both = chip + (n + 1) * (2 * ((j - 1) % 2) - 1)
        up = jnp.where(chip < chips - 1 - chip, j, chips - 1 - j)
        return jnp.where(j <= 2 * low, both, up) if j else chip

    def forward(j):
        s = nearest(j)
        for b in range(SUB):
            pass_on(s, b, False).wait_recv()
        final = j == chips - 1

        def one(t, carry):
            i = lax.rem(t // 2 + 1, outer_size)
            side = lax.rem(t, 2)
            ahead = outer_peer(i) * 2 + (1 - side) * (1 - inner) + side * inner
            left = tile_rows(ahead * blocks, blocks, s * 2 * blocks, 2 * blocks)
            right = source[pl.ds(pl.multiple_of(s * 2 * rows, rows), 2 * rows), :]
            total = jnp.dot(left, right, preferred_element_type=jnp.float32)
            if j > 0:
                total = total + jnp.concatenate([back[t, :, :width], back[t, :, width:]], axis=0)
            if not final:
                back[t, :, :width] = total[:half]
                back[t, :, width:] = total[half:]
                return carry

            back[t, :, :width] = total[:half]
            back[t, :, width:] = total[half:]

            @pl.when(side == 0)
            def _():
                near_send[i] = total[:half].astype(jnp.bfloat16)
                near_copy(i).start()

            @pl.when(i > 0)
            def _():
                far_send[i - 1, side] = total[half:].astype(jnp.bfloat16)
                far_copy(i, side).start()

            return carry

        lax.fori_loop(0, rep_size, one, 0)

    for j in range(chips):
        if j == chips - 1:
            for b in range(SUB):
                relay_source(chips - 2, b)
        forward(j)

    for i in range(1, outer_size):
        near_copy(i).wait_recv()
        far_send[i - 1, 2] = (
            back[2 * i - 1, :, :width] + near_recv[i].astype(jnp.float32)
        ).astype(jnp.bfloat16)
        far_copy(i, 2).start()
    for i in range(1, outer_size):
        far_copy(i, 0).wait_recv()
    beside = back[rep_size - 2, :, width:]
    for i in range(1, outer_size):
        beside = beside + far_recv[i - 1, 0].astype(jnp.float32)
    near_send[outer_size] = beside.astype(jnp.bfloat16)
    near_copy(outer_size).start()
    near_copy(0).wait_recv()
    upper = back[rep_size - 1, :, :width] + near_recv[0].astype(jnp.float32)
    lower = back[rep_size - 1, :, width:]
    for i in range(1, outer_size):
        far_copy(i, 1).wait_recv()
        lower = lower + far_recv[i - 1, 1].astype(jnp.float32)
    held[:half, :] = upper
    held[half:, :] = lower
    for i in range(1, outer_size):
        far_copy(i, 2).wait_recv()
    near_copy(outer_size).wait_recv()

    weight = weight_ref[...]
    slab = width // HALVES

    def finish(h, carry):
        lines = pl.ds(pl.multiple_of(h * 128, 128), 128)
        total = held[lines, :]
        piece = pl.ds(pl.multiple_of(lax.rem(h, half // 128) * 128, 128), 128)
        late = far_recv[0, 2, piece, :].astype(jnp.float32)
        for i in range(2, outer_size):
            late = late + far_recv[i - 1, 2, piece, :].astype(jnp.float32)
        total = total + jnp.where(h < half // 128, late, near_recv[outer_size, piece, :].astype(jnp.float32))
        high = total.astype(jnp.bfloat16)
        low = (total - high.astype(jnp.float32)).astype(jnp.bfloat16)
        summed = jnp.dot(high, weight, preferred_element_type=jnp.float32) + jnp.dot(
            low, weight, preferred_element_type=jnp.float32
        )
        sig = jax.nn.sigmoid(summed)
        out_ref[lines, :] = (summed * sig).astype(jnp.bfloat16)
        slope = sig * (1.0 + summed * (1.0 - sig))
        grad = (cot_ref[lines, :].astype(jnp.float32) * slope).astype(jnp.bfloat16)
        for h in range(HALVES):
            grads[h, 0, lines, :] = grad[:, h * slab : (h + 1) * slab]
        held[lines, :] = total
        return carry

    lax.fori_loop(0, rows // 128, finish, 0)

    def row_half(p):
        return pl.ds(p * half, half)

    def near_grad(h, i, p):
        k = h * (outer_size + 1) + (p if i == 0 else 1 + i)
        return pltpu.make_async_remote_copy(
            src_ref=grads.at[h, 2 * i, row_half(p)], dst_ref=grads.at[h, 2 * i + 1, row_half(p)],
            send_sem=near_gsend.at[k], recv_sem=near_grecv.at[k],
            device_id=(me_d, outer * 2 + 1 - inner), device_id_type=MESH,
        )

    def far_grad(h, i, side, p):
        k = (h * (outer_size - 1) + i - 1) * 3 + (2 if side else p)
        return pltpu.make_async_remote_copy(
            src_ref=grads.at[h, side, row_half(p)], dst_ref=grads.at[h, 2 * i + side, row_half(p)],
            send_sem=far_gsend.at[k], recv_sem=far_grecv.at[k],
            device_id=(me_d, outer_peer(i) * 2 + inner), device_id_type=MESH,
        )

    def spread_grads(h):
        for p in range(2):
            near_grad(h, 0, p).start()
            for i in range(1, outer_size):
                far_grad(h, i, 0, 1 - p).start()

    def relay_grads(h):
        near_grad(h, 0, 0).wait_recv()
        for i in range(1, outer_size):
            far_grad(h, i, 1, 0).start()
        for i in range(1, outer_size):
            far_grad(h, i, 0, 1).wait_recv()
            near_grad(h, i, 1).start()

    def grads_here(u, h):
        i = u // 2
        if u == 1:
            near_grad(h, 0, 1).wait_recv()
        elif u % 2:
            near_grad(h, i, 1).wait_recv()
            far_grad(h, i, 1, 0).wait_recv()
        elif u:
            far_grad(h, i, 0, 0).wait_recv()

    spread_grads(0)

    total = held[...]
    high = total.astype(jnp.bfloat16)
    low = (total - high.astype(jnp.float32)).astype(jnp.bfloat16)
    own_grad = jnp.concatenate([grads[h, 0] for h in range(HALVES)], axis=1)
    over_rows = (((0,), (0,)), ((), ()))
    own_term = lax.dot_general(high, own_grad, over_rows, preferred_element_type=jnp.float32)
    own_term = own_term + lax.dot_general(low, own_grad, over_rows, preferred_element_type=jnp.float32)
    gw2_send[...] = own_term
    gw1_send[...] = own_term.astype(jnp.bfloat16).reshape(dom_size, share, width)

    def gw1_copy(i):
        return pltpu.make_async_remote_copy(
            src_ref=gw1_send.at[dom_peer(i)], dst_ref=gw1_recv.at[i],
            send_sem=gw1_ssem.at[i], recv_sem=gw1_rsem.at[i],
            device_id=(dom_peer(i), me_r), device_id_type=MESH,
        )

    for i in range(1, dom_size):
        gw1_copy(i).start()

    def gw2_copy(i):
        return pltpu.make_async_remote_copy(
            src_ref=gw2_recv.at[me_r], dst_ref=gw2_recv.at[me_r],
            send_sem=gw2_ssem.at[i], recv_sem=gw2_rsem.at[i],
            device_id=(me_d, rep_peer(i)), device_id_type=MESH,
        )

    def gw3_copy(i):
        return pltpu.make_async_remote_copy(
            src_ref=gw3_recv.at[me_d], dst_ref=gw3_recv.at[me_d],
            send_sem=gw3_ssem.at[i], recv_sem=gw3_rsem.at[i],
            device_id=(dom_peer(i), me_r), device_id_type=MESH,
        )

    def weight_second():
        for i in range(1, dom_size):
            gw1_copy(i).wait_recv()
        mine = gw2_send[pl.ds(pl.multiple_of(me_d * share, share), share), :]
        for i in range(1, dom_size):
            mine = mine + gw1_recv[i].astype(jnp.float32)
        gw2_recv[me_r] = mine
        for i in range(1, rep_size):
            gw2_copy(i).start()

    def weight_third():
        for i in range(1, rep_size):
            gw2_copy(i).wait_recv()
        mine = gw2_recv[0]
        for i in range(1, rep_size):
            mine = mine + gw2_recv[i]
        gw3_recv[me_d] = mine.astype(jnp.bfloat16)
        for i in range(1, dom_size):
            gw3_copy(i).start()

    part = width // SPLIT
    each = SPLIT // HALVES
    hops = each * (chips - 1)

    def slab_of(h):
        return pl.ds(h * slab, slab)

    def back_step(u, h, flipped, d):
        from_outer = lax.rem(outer + outer_size - u // 2, outer_size)
        group = from_outer * 2 + (1 - inner if u % 2 else inner)
        right = tile_rows(group * blocks, blocks, d * blocks, blocks)
        product = jnp.dot(flipped, right, preferred_element_type=jnp.float32)
        if u > 0:
            product = back[d, slab_of(h), :] + product
        back[d, slab_of(h), :] = product

    def flip(u, h):
        return jnp.transpose(grads[h, u].astype(jnp.float32)).astype(jnp.bfloat16)

    def back_all(u, h):
        grads_here(u, h)
        flipped = flip(u, h)
        lax.fori_loop(0, dom_size, lambda d, c: (back_step(u, h, flipped, d), c)[1], 0)

    def turn(j):
        odd = lax.rem(j, 2)
        return (1 - odd) * (chips - 1 - j // 2) + odd * (j // 2)

    def pair_copy(j, h):
        there = turn(j)
        return pltpu.make_async_remote_copy(
            src_ref=back.at[there * 2 + 1 - core, slab_of(h)], dst_ref=pair.at[there, slab_of(h)],
            send_sem=pair_ssem.at[h * chips + j], recv_sem=pair_rsem.at[h * chips + j],
            device_id=(partner, me_r), device_id_type=MESH,
        )

    def up_copy(q, h):
        return pltpu.make_async_remote_copy(
            src_ref=up_send.at[h * hops + q], dst_ref=up_recv.at[h * hops + q],
            send_sem=up_ssem.at[h * hops + q], recv_sem=up_rsem.at[h * hops + q],
            device_id=((chip + 1) * 2 + core, me_r), device_id_type=MESH,
        )

    def down_copy(q, h):
        return pltpu.make_async_remote_copy(
            src_ref=down_send.at[h * hops + q], dst_ref=down_recv.at[h * hops + q],
            send_sem=down_ssem.at[h * hops + q], recv_sem=down_rsem.at[h * hops + q],
            device_id=((chip - 1) * 2 + core, me_r), device_id_type=MESH,
        )

    def own_part(there, q, h):
        lines = pl.ds(pl.multiple_of(h * slab + lax.rem(q, each) * part, part), part)
        return back[there * 2 + core, lines, :]

    def relay(tick, h):
        q_up = tick - chip
        q_down = tick - (chips - 1 - chip)

        @pl.when((chip > 0) & (q_up >= 0) & (q_up < each * (chips - 1 - chip)))
        def _():
            up_copy(q_up, h).wait_recv()
            up_send[h * hops + q_up] = (
                own_part(chips - 1 - q_up // each, q_up, h) + up_recv[h * hops + q_up].astype(jnp.float32)
            ).astype(jnp.bfloat16)
            up_copy(q_up, h).start()

        @pl.when((chip < chips - 1) & (q_down >= 0) & (q_down < each * chip))
        def _():
            down_copy(q_down, h).wait_recv()
            down_send[h * hops + q_down] = (
                own_part(q_down // each, q_down, h) + down_recv[h * hops + q_down].astype(jnp.float32)
            ).astype(jnp.bfloat16)
            down_copy(q_down, h).start()

    def relays(first, after, h):
        lax.fori_loop(first, after, lambda tick, c: (relay(tick, h), c)[1], 0)

    def back_last(h, between):
        u = rep_size - 1
        grads_here(u, h)
        flipped = flip(u, h)

        def toward(j, carry):
            back_step(u, h, flipped, turn(j) * 2 + 1 - core)
            pair_copy(j, h).start()
            return carry

        def keep(j, carry):
            there = turn(j)
            back_step(u, h, flipped, there * 2 + core)
            pair_copy(j, h).wait_recv()
            mine = there * 2 + core
            back[mine, slab_of(h), :] = back[mine, slab_of(h), :] + pair[there, slab_of(h), :]

            @pl.when((chip == 0) & (there > 0))
            def _():
                for i in range(each):
                    q = (chips - 1 - there) * each + i
                    up_send[h * hops + q] = own_part(there, q, h).astype(jnp.bfloat16)
                    up_copy(q, h).start()

            @pl.when((chip == chips - 1) & (there < chips - 1))
            def _():
                for i in range(each):
                    q = there * each + i
                    down_send[h * hops + q] = own_part(there, q, h).astype(jnp.bfloat16)
                    down_copy(q, h).start()

            return carry

        lax.fori_loop(0, chips, toward, 0)
        between()
        lax.fori_loop(0, chips, keep, 0)

    ticks = each * (chips - 2)
    back_all(0, 0)
    relay_grads(0)
    weight_second()
    for h in range(1, HALVES):
        spread_grads(h)
    for u in range(1, rep_size - 1):
        back_all(u, 0)
    back_last(0, weight_third)
    for h in range(1, HALVES):
        relay_grads(h)
        for u in range(rep_size - 1):
            back_all(u, h)
            relays(1 + ticks * u // rep_size, 1 + ticks * (u + 1) // rep_size, h - 1)
        back_last(h, lambda: relays(1 + ticks * (rep_size - 1) // rep_size, 1 + ticks, h - 1))
    relays(1, 1 + ticks, HALVES - 1)

    for h in range(HALVES):
        for i in range(each):
            lines = pl.ds(h * slab + i * part, part)

            @pl.when(chip > 0)
            def _():
                q = (chips - 1 - chip) * each + i
                up_copy(q, h).wait_recv()
                back[me_d, lines, :] = back[me_d, lines, :] + up_recv[h * hops + q].astype(jnp.float32)

            @pl.when(chip < chips - 1)
            def _():
                q = chip * each + i
                down_copy(q, h).wait_recv()
                back[me_d, lines, :] = back[me_d, lines, :] + down_recv[h * hops + q].astype(jnp.float32)

            gp_ref[lines, :] = back[me_d, lines, :].astype(jnp.bfloat16)

    for i in range(1, dom_size):
        gw3_copy(i).wait_recv()
    gw_ref[...] = gw3_recv[...].reshape(width, width)
    for i in range(outer_size + 1):
        near_copy(i).wait_send()
    for i in range(1, outer_size):
        for k in range(3):
            far_copy(i, k).wait_send()
    for u in range(1, rep_size):
        gw2_copy(u).wait_send()
    for i in range(1, dom_size):
        gw1_copy(i).wait_send()
        gw3_copy(i).wait_send()
    for h in range(HALVES):
        for p in range(2):
            near_grad(h, 0, p).wait_send()
        for i in range(1, outer_size):
            near_grad(h, i, 1).wait_send()
            far_grad(h, i, 0, 0).wait_send()
            far_grad(h, i, 0, 1).wait_send()
            far_grad(h, i, 1, 0).wait_send()
        for j in range(chips):
            pair_copy(j, h).wait_send()

    def sent(q, carry):
        for h in range(HALVES):

            @pl.when((chip < chips - 1) & (q < each * (chips - 1 - chip)))
            def _():
                up_copy(q, h).wait_send()

            @pl.when((chip > 0) & (q < each * chip))
            def _():
                down_copy(q, h).wait_send()

        return carry

    lax.fori_loop(0, hops, sent, 0)

    for n in range(chips - 1):
        for b in range(SUB):

            @pl.when((chip < chips - 1) & (chip - n >= 0))
            def _():
                lift(n, b).wait_send()

            @pl.when((chip > 0) & (chip + n < chips))
            def _():
                sink(n, b).wait_send()

    for s in range(chips):
        for b in range(SUB):
            pass_on(s, b, False).wait_send()


def finish_kernel(raw_ref, gp_ref, gw_in_ref, weight_ref, out_ref, gf_ref, gw_ref):
    out_ref[...] = raw_ref[...]
    gw_ref[...] = gw_in_ref[...].astype(jnp.float32)
    grad_projected = jnp.transpose(gp_ref[...])
    gf_ref[...] = lax.dot_general(
        grad_projected, weight_ref[...], (((1,), (1,)), ((), ())), preferred_element_type=jnp.float32
    ).astype(jnp.bfloat16)


def finish(raw, grad_projected, grad_weight, weight):
    here = pl.BlockSpec(memory_space=pltpu.VMEM)
    return pl.pallas_call(
        finish_kernel,
        out_shape=(
            jax.ShapeDtypeStruct(raw.shape, jnp.bfloat16),
            jax.ShapeDtypeStruct(raw.shape, jnp.bfloat16),
            jax.ShapeDtypeStruct(grad_weight.shape, jnp.float32),
        ),
        in_specs=[here] * 4,
        out_specs=(here, here, here),
        name="finish",
        compiler_params=pltpu.CompilerParams(vmem_limit_bytes=16 * 2**20),
    )(raw, grad_projected, grad_weight, weight)


def room(scratch, extra):
    total = 0
    for item in scratch:
        if getattr(item, "memory_space", None) == pltpu.VMEM:
            size = jnp.dtype(item.dtype).itemsize
            for length in item.shape:
                size *= length
            total += size
    return total + extra


def run_layer(count, features, weight, cotangent, row_index, col_index, tiles, dom_size, rep_size):
    rows, width = cotangent.shape
    chips = dom_size // 2
    share = width // dom_size
    slots = tiles.shape[0]
    places = dom_size * rep_size * (rows // TILE) ** 2
    assert rows == 2 * width and rep_size <= dom_size
    here = pl.BlockSpec(memory_space=pltpu.VMEM)
    away = pl.BlockSpec(memory_space=pltpu.HBM)
    sems = lambda count: pltpu.SemaphoreType.DMA((count,))
    half, full, whole = jnp.bfloat16, jnp.float32, jnp.int32
    hops = SPLIT * (chips - 1)
    walks = SUB * (chips - 1)
    scratch = [
        pltpu.VMEM((dom_size * rows, width), half),
        pltpu.VMEM((slots, TILE, TILE), half),
        pltpu.VMEM((slots + 1, TILE, TILE), half),
        pltpu.VMEM((width, width), half),
        pltpu.VMEM((rows, width), half),
        pltpu.VMEM((1, slots), whole),
        pltpu.VMEM((1, slots), whole),
        pltpu.VMEM((1, slots), whole),
        pltpu.VMEM((1, slots), whole),
        pltpu.VMEM((1, places), whole),
        pltpu.SMEM((1, slots), whole),
        pltpu.SMEM((1, slots), whole),
        pltpu.SMEM((1, places), whole),
        pltpu.VMEM((rep_size // 2 + 1, rows // 2, width), half),
        pltpu.VMEM((rep_size // 2 + 1, rows // 2, width), half),
        pltpu.VMEM((rep_size // 2 - 1, 3, rows // 2, width), half),
        pltpu.VMEM((rep_size // 2 - 1, 3, rows // 2, width), half),
        pltpu.VMEM((rows, width), full),
        pltpu.VMEM((HALVES, rep_size, rows, width // HALVES), half),
        pltpu.VMEM((dom_size, width, rows), full),
        pltpu.VMEM((chips, width, rows), full),
        pltpu.VMEM((hops, width // SPLIT, rows), half),
        pltpu.VMEM((hops, width // SPLIT, rows), half),
        pltpu.VMEM((hops, width // SPLIT, rows), half),
        pltpu.VMEM((hops, width // SPLIT, rows), half),
        pltpu.VMEM((dom_size, share, width), half),
        pltpu.VMEM((dom_size, share, width), half),
        pltpu.VMEM((width, width), full),
        pltpu.VMEM((rep_size, share, width), full),
        pltpu.VMEM((dom_size, share, width), half),
        sems(LOADS), sems(5), sems(3), sems(walks), sems(walks), sems(walks), sems(walks),
        sems(SUB * chips), sems(SUB * chips),
        sems(rep_size // 2 + 1), sems(rep_size // 2 + 1), sems(3 * (rep_size // 2 - 1)), sems(3 * (rep_size // 2 - 1)),
        sems(HALVES * (rep_size // 2 + 1)), sems(HALVES * (rep_size // 2 + 1)),
        sems(HALVES * 3 * (rep_size // 2 - 1)), sems(HALVES * 3 * (rep_size // 2 - 1)),
        sems(HALVES * chips), sems(HALVES * chips), sems(hops), sems(hops), sems(hops), sems(hops),
        sems(dom_size), sems(dom_size), sems(rep_size), sems(rep_size),
        sems(dom_size), sems(dom_size),
    ]
    return pl.pallas_call(
        functools.partial(layer_kernel, dom_size, rep_size),
        out_shape=(
            jax.ShapeDtypeStruct((rows, width), half),
            jax.ShapeDtypeStruct((width, rows), half),
            jax.ShapeDtypeStruct((width, width), half),
        ),
        in_specs=[pl.BlockSpec(memory_space=pltpu.SMEM)] + [away] * 6,
        out_specs=(here, here, here),
        scratch_shapes=scratch,
        name="layer",
        compiler_params=pltpu.CompilerParams(
            collective_id=0, has_side_effects=True, vmem_limit_bytes=min(room(scratch, 6 * 2**20), 67043328)
        ),
    )(count, features, weight, cotangent, row_index, col_index, tiles)


def body(node_features, weight, cotangent, tile_row, tile_col, tile_values, tile_count):
    dom_size = lax.axis_size("dom")
    rep_size = lax.axis_size("rep")
    slots = tile_row.shape[2]
    raw, grad_projected, grad_weight = run_layer(
        tile_count.reshape(1),
        node_features,
        weight,
        cotangent,
        tile_row.reshape(1, slots),
        tile_col.reshape(1, slots),
        tile_values.reshape(slots, TILE, TILE),
        dom_size,
        rep_size,
    )
    return tuple(finish(raw, grad_projected, grad_weight, weight))


def solution(mesh):
    placed = (
        P(("dom", "rep"), None),
        P(),
        P(("dom", "rep"), None),
        P("dom", "rep", None),
        P("dom", "rep", None),
        P("dom", "rep", None, None, None),
        P("dom", "rep"),
    )
    return jax.shard_map(
        body,
        mesh=mesh,
        in_specs=placed,
        out_specs=(P(("dom", "rep"), None), P(("dom", "rep"), None), P()),
        check_vma=False,
    )
```
